768 devices in a mesh: ctx: 192 (over z, y_lo, x), head: 4 (over y_hi, core).
Axes of the slice: x: 4, y: 8 (y_hi: 2, y_lo: 4; y = y_hi * 4 + y_lo), z: 12, core: 2. Of those that a mesh axis runs over, the one named last changes fastest.
Arguments:
- hidden: bfloat16 [98304, 4096], P('ctx'), may hold values from -20 to 20
- w_query: bfloat16 [4096, 2048], P(None, 'head'), may hold values from -2 to 2
- key_projection: bfloat16 [4096, 512], P(None, 'head'), may hold values from -2 to 2
- value_projection: bfloat16 [4096, 512], P(None, 'head'), may hold values from -0.09375 to 0.09375
- q_gain: float32 [128], replicated, may hold values from 0.5 to 5
- key_norm_gain: float32 [128], replicated, may hold values from 0.5 to 5
- starts: int32 [384], replicated, may hold values from 0 to 98048, as said below
Outputs:
- attended: bfloat16 [98304, 2048], P(('ctx', 'head'))
The draws below stay inside these ranges and needn't reach their ends.
Inputs may be any that keep to these rules, and one draw needn't show every extreme that they name: starts is 256 times a permutation of 0 to 383.
All inputs are finite; a program needn't handle non-finite values.
Results may differ from the reference program's by a relative error of at most 0.0085.
The reference program's roundings to bfloat16 on the way count: a program that leaves them out, or rounds other values in their place, can miss the bound.
Values may be sent and summed in bfloat16 or wider, within the bound.
A program may use at most 32 MiB of HBM per device.

```python
import jax
import jax.numpy as jnp
from jax import lax

MODEL_WIDTH = 4096
HQ = 16
KEY_VALUE_HEADS = 4
HEAD_SIZE = 128
BLK = 512
HALF = 256
SEQ = 98304
N_CTX = 192


def draw_hidden(key, part):
    noise_rows = jnp.clip(jax.random.normal(jax.random.fold_in(key, 103), (SEQ, MODEL_WIDTH), jnp.float32), -6.0, 6.0)
    return noise_rows.astype(jnp.bfloat16)


def matched_weight(key, salt, heads):
    drawn = jnp.clip(jax.random.normal(jax.random.fold_in(key, salt), (MODEL_WIDTH, heads * HEAD_SIZE), jnp.float32), -5.0, 5.0)
    drawn = drawn / jnp.sqrt(jnp.float32(MODEL_WIDTH))
    return drawn.astype(jnp.bfloat16)


def draw_w_query(key, part):
    return matched_weight(key, 109, HQ)


def draw_key_projection(key, part):
    return matched_weight(key, 113, KEY_VALUE_HEADS)


def gain_values(key, salt):
    other = jax.random.fold_in(key, salt)
    return jax.random.uniform(other, (HEAD_SIZE,), jnp.float32, 0.5, 2.0)


def draw_q_gain(key, part):
    return gain_values(key, 5)


def draw_key_norm_gain(key, part):
    return gain_values(key, 7)


def draw_starts(key, part):
    order = jax.random.permutation(jax.random.fold_in(key, 11), 2 * N_CTX)
    return (order * HALF).astype(jnp.int32)


def steps_of(stream_key, shape, cuts, low, largest):
    factor_of, own = 1.0, jax.random.fold_in(stream_key, 6)
    for axis_at, parts in cuts:
        steps = jnp.exp(jax.random.uniform(jax.random.fold_in(own, axis_at), (parts,), jnp.float32, low / len(cuts), largest / len(cuts)))
        factor_of = factor_of * jnp.repeat(steps, shape[axis_at] // parts).reshape([-1 if axis == axis_at else 1 for axis in range(len(shape))])
    return factor_of


def centred(key, shape, deviation, limit, pieces=(), kind=jnp.bfloat16):
    entries = jax.random.normal(key, shape, jnp.float32) * deviation
    if len(pieces) > 0:
        entries = steps_of(key, shape, pieces, -0.22, 0.18) * entries
    return jnp.clip(entries, min=-limit, max=limit).astype(kind)


def setup_inputs(seed: int = 0) -> dict:
    arg_keys = jax.random.split(jax.random.key(seed), 8)
    hidden = draw_hidden(jax.random.fold_in(arg_keys[7], 71), 0)
    w_query = draw_w_query(jax.random.fold_in(arg_keys[7], 71), 0)
    key_projection = draw_key_projection(jax.random.fold_in(arg_keys[7], 71), 0)
    value_projection = centred(arg_keys[3], (MODEL_WIDTH, KEY_VALUE_HEADS * HEAD_SIZE), MODEL_WIDTH ** -0.5, 0.09375, ((1, 4),))
    q_gain = draw_q_gain(jax.random.fold_in(arg_keys[7], 71), 0)
    key_norm_gain = draw_key_norm_gain(jax.random.fold_in(arg_keys[7], 71), 0)
    starts = draw_starts(jax.random.fold_in(arg_keys[7], 71), 0)
    return dict(hidden=hidden, w_query=w_query, key_projection=key_projection, value_projection=value_projection, q_gain=q_gain, key_norm_gain=key_norm_gain, starts=starts)


def rms_scaled(rows, weight):
    return rows * lax.rsqrt(lax.optimization_barrier(jnp.mean(rows * rows, axis=-1, keepdims=True)) + 1e-06) * weight

def rotated(rows, positions):
    width = rows.shape[-1] // 2
    freqs = jnp.power(jnp.float32(1000000.0), -jnp.arange(width, dtype=jnp.float32) * 2.0 / (2 * width))
    angles = positions.astype(jnp.float32)[:, None] * freqs[None, :]
    cosine = jnp.cos(angles)[:, None, :]
    sine = jnp.sin(angles)[:, None, :]
    first = rows[..., :width]
    second = rows[..., width:]
    return jnp.concatenate([first * cosine - second * sine, second * cosine + first * sine], axis=-1)

def projected_rows(hidden, weight, gain, positions, heads):
    rows = jnp.dot(hidden, weight, preferred_element_type=jnp.float32)
    rows = rows.reshape(hidden.shape[0], heads, -1)
    return rotated(rms_scaled(rows, gain), positions).astype(jnp.bfloat16)

def block_positions(starts, index, half_len):
    pair = lax.dynamic_slice(starts, (2 * index,), (2,))
    offsets = jnp.arange(2 * half_len, dtype=jnp.int32)
    return jnp.where(offsets < half_len, pair[0] + offsets, pair[1] + offsets - half_len)

def attend(queries, key_rows, value_rows, q_pos, k_pos):
    count, q_heads, head_dim = queries.shape
    kv_heads = key_rows.shape[1]
    grouped = queries.reshape(count, kv_heads, q_heads // kv_heads, head_dim)
    scores = jnp.einsum('qkgd,skd->kgqs', grouped.astype(jnp.float32), key_rows.astype(jnp.float32)) * head_dim ** (-0.5)
    visible = k_pos[None, :] <= q_pos[:, None]
    scores = jnp.where(visible[None, None], scores, -1e+30)
    top = lax.optimization_barrier(jnp.max(scores, axis=-1, keepdims=True))
    weights = jnp.exp(scores - top)
    weights = (weights / lax.optimization_barrier(jnp.sum(weights, axis=-1, keepdims=True))).astype(jnp.bfloat16)
    output = jnp.einsum('kgqs,skd->qkgd', weights.astype(jnp.float32), value_rows.astype(jnp.float32))
    return output.reshape(count, q_heads * head_dim).astype(jnp.bfloat16)

def reference(hidden, w_query, key_projection, value_projection, q_gain, key_norm_gain, starts):
    half_len = BLK // 2
    block_ids = jnp.arange(N_CTX, dtype=jnp.int32)
    every_position = lax.map(lambda index: block_positions(starts, index, half_len), block_ids).reshape(-1)
    queries = projected_rows(hidden, w_query, q_gain, every_position, HQ)
    rotated_keys = projected_rows(hidden, key_projection, key_norm_gain, every_position, KEY_VALUE_HEADS)
    value_rows = jnp.dot(hidden, value_projection, preferred_element_type=jnp.float32).astype(jnp.bfloat16).reshape(-1, KEY_VALUE_HEADS, HEAD_SIZE)

    def rows_of(array, block):
        return lax.dynamic_slice_in_dim(array, (block * BLK).astype(jnp.int32), BLK, 0)

    def one_block(index):
        near = (index + N_CTX - 1) % N_CTX
        far = (index + N_CTX - 2) % N_CTX
        key_all = jnp.concatenate([rows_of(rotated_keys, index), rows_of(rotated_keys, near), rows_of(rotated_keys, far)], axis=0)
        val_all = jnp.concatenate([rows_of(value_rows, index), rows_of(value_rows, near), rows_of(value_rows, far)], axis=0)
        pos_all = jnp.concatenate([rows_of(every_position, index), rows_of(every_position, near), rows_of(every_position, far)], axis=0)
        return attend(rows_of(queries, index), key_all, val_all, rows_of(every_position, index), pos_all)
    output = lax.map(one_block, block_ids)
    return output.reshape(SEQ, HQ * HEAD_SIZE)
```

```python
import functools

import jax
import jax.numpy as jnp
import numpy as np
from jax import lax
from jax.experimental import pallas as pl
from jax.experimental.pallas import tpu as pltpu
from jax.sharding import PartitionSpec as P

MESH = pl.DeviceIdType.MESH
NEG = -1e30
F32 = jnp.float32
BF16 = jnp.bfloat16


def half_pi_parts():
    rest, parts = np.pi / 2, []
    for _ in range(3):
        unit = 2.0 ** (np.floor(np.log2(rest)) - 7)
        parts.append(float(np.floor(rest / unit) * unit))
        rest -= parts[-1]
    return parts + [float(np.float32(rest))]


def cos_sin(angle, is_cos):
    turns = jnp.floor(angle * np.float32(2 / np.pi) + 0.5)
    r = angle
    for part in half_pi_parts():
        r = r - turns * np.float32(part)
    r2 = r * r
    s = r + r * r2 * (
        np.float32(-1.6666654611e-1)
        + r2 * (np.float32(8.3321608736e-3) + r2 * np.float32(-1.9515295891e-4))
    )
    c = 1.0 - 0.5 * r2 + r2 * r2 * (
        np.float32(4.166664568298827e-2)
        + r2 * (np.float32(-1.388731625493765e-3) + r2 * np.float32(2.443315711809948e-5))
    )
    quadrant = turns.astype(jnp.int32) + jnp.where(is_cos, 0, 3)
    value = jnp.where((quadrant & 1) == 0, c, s)
    return jnp.where(((quadrant + 1) & 2) == 0, value, -value)


def kernel(
    n_ctx, hid, wq, wk, wv, gq, gk, freq, starts, out,
    hbuf, wqb, wkvb, cosb, sinb, kv, q, acc, top, tot, att,
    in_sem, kv_send, kv_recv, out_send, out_recv, own_sem,
):
    c = lax.axis_index("ctx")
    h = lax.axis_index("head")
    blk, width = hid.shape
    half = blk // 2
    heads = wq.shape[1] // 128
    rows = blk // 4
    grp = heads * rows
    chunks = 4
    step = width // chunks

    def ctx_at(d):
        return lax.rem(c + (d + n_ctx), n_ctx)

    y_hi, core = h // 2, lax.rem(h, 2)
    far_same = (1 - y_hi) * 2 + core
    far_other = (1 - y_hi) * 2 + 1 - core
    near_other = y_hi * 2 + 1 - core
    peers = (far_same, far_other, near_other)

    barrier = pltpu.get_barrier_semaphore()
    for d in (1, 2, -1, -2):
        pl.semaphore_signal(barrier, inc=1, device_id=(ctx_at(d), h), device_id_type=MESH)
    for peer in peers:
        pl.semaphore_signal(barrier, inc=1, device_id=(c, peer), device_id_type=MESH)

    loads = []
    for i in range(chunks):
        part = pl.ds(i * step, step)
        loads.append([
            pltpu.make_async_copy(hid.at[:, part], hbuf.at[:, part], in_sem.at[4 * i]),
            pltpu.make_async_copy(wk.at[part], wkvb.at[part, pl.ds(0, 128)], in_sem.at[4 * i + 1]),
            pltpu.make_async_copy(wv.at[part], wkvb.at[part, pl.ds(128, 128)], in_sem.at[4 * i + 2]),
        ])
    q_loads = [
        pltpu.make_async_copy(
            wq.at[pl.ds(i * step, step)], wqb.at[pl.ds(i * step, step)], in_sem.at[4 * i + 3]
        )
        for i in range(chunks)
    ]
    for group in loads:
        for load in group:
            load.start()
    for load in q_loads:
        load.start()

    lane = lax.broadcasted_iota(jnp.int32, (blk, 128), 1)
    token = lax.broadcasted_iota(jnp.int32, (blk, 128), 0)
    start = [starts[2 * c], starts[2 * c + 1]]
    pos = jnp.where(token < half, start[0] + token, start[1] + token - half)
    first = lane < 64
    table = cos_sin(pos.astype(F32) * freq[...], first)
    turned = pltpu.roll(table, 64, 1)
    cosb[...] = jnp.where(first, table, turned)
    sinb[...] = jnp.where(first, -turned, table)

    def normed(x, gain):
        x = x * lax.rsqrt(jnp.mean(x * x, axis=-1, keepdims=True) + 1e-6) * gain
        return x * cosb[...] + pltpu.roll(x, 64, 1) * sinb[...]

    total = None
    for i in range(chunks):
        for load in loads[i]:
            load.wait()
        part = pl.ds(i * step, step)
        term = jnp.dot(hbuf[:, part], wkvb[part, :], preferred_element_type=F32)
        total = term if total is None else total + term
    kv[0, 1] = total[:, 128:].astype(BF16)
    kv[0, 0] = normed(total[:, :128], gk[...]).astype(BF16)

    pl.semaphore_wait(barrier, 7)
    kv_copies = {}
    for d in (1, 2):
        for s in (0, 1):
            i = 2 * (d - 1) + s
            kv_copies[d, s] = pltpu.make_async_remote_copy(
                src_ref=kv.at[0, s],
                dst_ref=kv.at[d, s],
                send_sem=kv_send.at[i],
                recv_sem=kv_recv.at[i],
                device_id=(ctx_at(d), h),
                device_id_type=MESH,
            )
            kv_copies[d, s].start()

    qsum = None
    for i in range(chunks):
        q_loads[i].wait()
        part = pl.ds(i * step, step)
        term = jnp.dot(hbuf[:, part], wqb[part, :], preferred_element_type=F32)
        qsum = term if qsum is None else qsum + term
    for j in range(heads):
        rotated = normed(qsum[:, j * 128 : (j + 1) * 128], gq[...]).astype(BF16)
        for g in range(4):
            q[pl.ds(g * grp + j * rows, rows), :] = rotated[g * rows : (g + 1) * rows]

    factor = np.float32(128 ** (-0.5) * np.log2(np.e))
    tiles = blk // 128

    def scores(g, d):
        return lax.dot_general(
            q[pl.ds(g * grp, grp), :], kv[d, 0], (((1,), (1,)), ((), ())),
            preferred_element_type=F32,
        )

    def lane_fold(op, x):
        folded = x[:, :128]
        for i in range(1, tiles):
            folded = op(folded, x[:, i * 128 : (i + 1) * 128])
        return folded

    def weigh(p, d):
        return jnp.dot(p.astype(BF16), kv[d, 1], preferred_element_type=F32)

    def q_start(g):
        return jnp.where(g < 2, start[0], start[1])

    def own(g, _):
        at = pl.ds(pl.multiple_of(g * grp, grp), grp)
        s = scores(g, 0)
        key = lax.broadcasted_iota(jnp.int32, (rows, blk), 1)
        k_pos = jnp.where(key < half, start[0] + key, start[1] + key - half)
        q_pos = q_start(g) + lax.rem(g, 2) * rows + lax.broadcasted_iota(jnp.int32, (rows, blk), 0)
        seen = k_pos <= q_pos
        for j in range(heads):
            a = pl.ds(pl.multiple_of(g * grp + j * rows, rows), rows)
            sj = jnp.where(seen, s[j * rows : (j + 1) * rows], NEG)
            m = jnp.max(lane_fold(jnp.maximum, sj), axis=-1, keepdims=True)
            p = jnp.exp2((sj - m) * factor)
            top[a, :] = jnp.broadcast_to(m, (rows, 128))
            tot[a, :] = lane_fold(jnp.add, p)
            acc[a, :] = weigh(p, 0)
        return 0

    def biases(g, d):
        return [
            jnp.where(starts[2 * ctx_at(-d) + i] <= q_start(g), np.float32(0), np.float32(NEG))
            for i in range(2)
        ]

    def further(g, d, finish):
        s = scores(g, d)
        bias = biases(g, d)
        for j in range(heads):
            a = pl.ds(pl.multiple_of(g * grp + j * rows, rows), rows)
            sj = s[j * rows : (j + 1) * rows]
            left, right = sj[:, :half], sj[:, half:]
            peak = jnp.maximum(
                jnp.maximum(left[:, :128], left[:, 128:]) + bias[0],
                jnp.maximum(right[:, :128], right[:, 128:]) + bias[1],
            )
            old = top[a, :]
            new = jnp.maximum(old, jnp.max(peak, axis=-1, keepdims=True))
            m = new[:, :1]
            p = jnp.concatenate(
                [jnp.exp2((left - (m - bias[0])) * factor), jnp.exp2((right - (m - bias[1])) * factor)],
                axis=1,
            )
            keep = jnp.exp2((old - new) * factor)
            tot_new = tot[a, :] * keep + lane_fold(jnp.add, p)
            acc_new = acc[a, :] * keep + weigh(p, d)
            if finish is None:
                top[a, :], tot[a, :], acc[a, :] = new, tot_new, acc_new
            else:
                denom = jnp.sum(tot_new, axis=-1, keepdims=True)
                finish(j, (acc_new / denom).astype(BF16))

    lax.fori_loop(0, 4, own, 0)

    kv_copies[1, 0].wait_recv()
    kv_copies[1, 1].wait_recv()

    def near(g, _):
        further(g, 1, None)
        return 0

    lax.fori_loop(0, 4, near, 0)

    kv_copies[2, 0].wait_recv()
    kv_copies[2, 1].wait_recv()
    mine = pl.ds(pl.multiple_of(h * heads * 128, heads * 128), heads * 128)

    def target(t):
        return jnp.where(t == 0, far_same, jnp.where(t == 1, far_other, jnp.where(t == 2, near_other, h)))

    def result_copy(t):
        return pltpu.make_async_remote_copy(
            src_ref=att.at[t],
            dst_ref=out.at[:, mine],
            send_sem=out_send.at[t],
            recv_sem=out_recv.at[t],
            device_id=(c, target(t)),
            device_id_type=MESH,
        )

    def last(t, _):
        def finish(j, value):
            att[t, :, j * 128 : (j + 1) * 128] = value

        further(target(t), 2, finish)

        @pl.when(t < 3)
        def _():
            result_copy(t).start()

        return 0

    lax.fori_loop(0, 4, last, 0)
    own_copy = pltpu.make_async_copy(att.at[3], out.at[:, mine], own_sem)
    own_copy.start()
    for copy in kv_copies.values():
        copy.wait_send()
    own_copy.wait()
    for t in range(3):
        result_copy(jnp.int32(t)).wait()


def solution(mesh):
    n_ctx = mesh.shape["ctx"]

    def shards(hidden, w_query, key_projection, value_projection, q_gain, key_norm_gain, starts):
        blk, width = hidden.shape
        cols = w_query.shape[1]
        rows = blk // 4
        freqs = jnp.power(F32(1000000.0), -jnp.arange(64, dtype=F32) * 2.0 / 128)
        freqs = jnp.concatenate([freqs, freqs]).reshape(1, 128)
        any_ = pl.BlockSpec(memory_space=pl.ANY)
        vmem = pl.BlockSpec(memory_space=pltpu.VMEM)
        n_rows = rows * 4 * (cols // 128)
        return pl.pallas_call(
            functools.partial(kernel, n_ctx),
            out_shape=jax.ShapeDtypeStruct((rows, cols * 4), BF16),
            in_specs=[any_] * 4 + [vmem] * 3 + [pl.BlockSpec(memory_space=pltpu.SMEM)],
            out_specs=any_,
            scratch_shapes=[
                pltpu.VMEM((blk, width), BF16),
                pltpu.VMEM((width, cols), BF16),
                pltpu.VMEM((width, 256), BF16),
                pltpu.VMEM((blk, 128), F32),
                pltpu.VMEM((blk, 128), F32),
                pltpu.VMEM((3, 2, blk, 128), BF16),
                pltpu.VMEM((n_rows, 128), BF16),
                pltpu.VMEM((n_rows, 128), F32),
                pltpu.VMEM((n_rows, 128), F32),
                pltpu.VMEM((n_rows, 128), F32),
                pltpu.VMEM((4, rows, cols), BF16),
                pltpu.SemaphoreType.DMA((16,)),
                pltpu.SemaphoreType.DMA((4,)),
                pltpu.SemaphoreType.DMA((4,)),
                pltpu.SemaphoreType.DMA((3,)),
                pltpu.SemaphoreType.DMA((3,)),
                pltpu.SemaphoreType.DMA,
            ],
            compiler_params=pltpu.CompilerParams(
                collective_id=0, has_side_effects=True, vmem_limit_bytes=60 << 20
            ),
        )(
            hidden, w_query, key_projection, value_projection,
            q_gain.reshape(1, 128), key_norm_gain.reshape(1, 128), freqs, starts,
        )

    return jax.shard_map(
        shards,
        mesh=mesh,
        in_specs=(P("ctx", None), P(None, "head"), P(None, "head"), P(None, "head"), P(), P(), P()),
        out_specs=P(("ctx", "head"), None),
        check_vma=False,
    )
```

```python
import functools

import jax
import jax.numpy as jnp
import numpy as np
from jax import lax
from jax.experimental import pallas as pl
from jax.experimental.pallas import tpu as pltpu
from jax.sharding import PartitionSpec as P

MESH = pl.DeviceIdType.MESH
NEG = -1e30
F32 = jnp.float32
BF16 = jnp.bfloat16


def half_pi_parts():
    rest, parts = np.pi / 2, []
    for _ in range(3):
        unit = 2.0 ** (np.floor(np.log2(rest)) - 7)
        parts.append(float(np.floor(rest / unit) * unit))
        rest -= parts[-1]
    return parts + [float(np.float32(rest))]


def cos_sin(angle, is_cos):
    turns = jnp.floor(angle * np.float32(2 / np.pi) + 0.5)
    r = angle
    for part in half_pi_parts():
        r = r - turns * np.float32(part)
    r2 = r * r
    s = r + r * r2 * (
        np.float32(-1.6666654611e-1)
        + r2 * (np.float32(8.3321608736e-3) + r2 * np.float32(-1.9515295891e-4))
    )
    c = 1.0 - 0.5 * r2 + r2 * r2 * (
        np.float32(4.166664568298827e-2)
        + r2 * (np.float32(-1.388731625493765e-3) + r2 * np.float32(2.443315711809948e-5))
    )
    quadrant = turns.astype(jnp.int32) + jnp.where(is_cos, 0, 3)
    value = jnp.where((quadrant & 1) == 0, c, s)
    return jnp.where(((quadrant + 1) & 2) == 0, value, -value)


def kernel(
    n_ctx, hid, wq, wk, wv, gq, gk, freq, starts, out,
    hbuf, wqb, wkvb, cosb, sinb, kv, q, acc, top, tot, att,
    w_sem, h_sem, q_sem, kv_send, kv_recv, out_send, out_recv, own_sem,
):
    c = lax.axis_index("ctx")
    h = lax.axis_index("head")
    blk, width = hid.shape
    half = blk // 2
    heads = wq.shape[1] // 128
    rows = blk // 4
    grp = heads * rows
    chunks = 4
    step = width // chunks

    def ctx_at(d):
        return lax.rem(c + (d + n_ctx), n_ctx)

    x = lax.rem(c, 4)
    y_hi, core = h // 2, lax.rem(h, 2)
    peers = (
        (1 - y_hi) * 2 + core,
        (1 - y_hi) * 2 + 1 - core,
        y_hi * 2 + 1 - core,
        h,
    )

    barrier = pltpu.get_barrier_semaphore()
    for d in (-1, jnp.where(x == 0, 1, jnp.where(x == 1, -3, -2))):
        pl.semaphore_signal(barrier, inc=1, device_id=(ctx_at(d), h), device_id_type=MESH)
    for peer in peers[:3]:
        pl.semaphore_signal(barrier, inc=1, device_id=(c, peer), device_id_type=MESH)

    parts = [pl.ds(i * step, step) for i in range(chunks)]
    halves = [pl.ds(0, half), pl.ds(half, half)]
    w_loads = [
        (
            pltpu.make_async_copy(wk.at[part], wkvb.at[part, pl.ds(0, 128)], w_sem.at[2 * i]),
            pltpu.make_async_copy(wv.at[part], wkvb.at[part, pl.ds(128, 128)], w_sem.at[2 * i + 1]),
        )
        for i, part in enumerate(parts)
    ]
    h_loads = [
        [
            pltpu.make_async_copy(
                hid.at[tokens, part], hbuf.at[tokens, part], h_sem.at[n * chunks + i]
            )
            for i, part in enumerate(parts)
        ]
        for n, tokens in enumerate(halves)
    ]
    q_loads = [
        pltpu.make_async_copy(wq.at[part], wqb.at[part], q_sem.at[i])
        for i, part in enumerate(parts)
    ]
    for i in range(chunks):
        w_loads[i][0].start()
        w_loads[i][1].start()
        h_loads[0][i].start()
    for load in h_loads[1] + q_loads:
        load.start()

    lane = lax.broadcasted_iota(jnp.int32, (blk, 128), 1)
    token = lax.broadcasted_iota(jnp.int32, (blk, 128), 0)
    start = [starts[2 * c], starts[2 * c + 1]]
    pos = jnp.where(token < half, start[0] + token, start[1] + token - half)
    first = lane < 64
    table = cos_sin(pos.astype(F32) * freq[...], first)
    turned = pltpu.roll(table, 64, 1)
    cosb[...] = jnp.where(first, table, turned)
    sinb[...] = jnp.where(first, -turned, table)

    def normed(x, gain, tokens):
        x = x * lax.rsqrt(jnp.mean(x * x, axis=-1, keepdims=True) + 1e-6) * gain
        return x * cosb[tokens, :] + pltpu.roll(x, 64, 1) * sinb[tokens, :]

    def near_copy(n, s):
        i = 2 * n + s
        return pltpu.make_async_remote_copy(
            src_ref=kv.at[s, pl.ds(n * half, half)],
            dst_ref=kv.at[s, pl.ds(blk + n * half, half)],
            send_sem=kv_send.at[i],
            recv_sem=kv_recv.at[i],
            device_id=(ctx_at(1), h),
            device_id_type=MESH,
        )

    def second_copy(n, s):
        i = 2 * n + s
        over = (x == 2).astype(jnp.int32)
        return pltpu.make_async_remote_copy(
            src_ref=kv.at[s, pl.ds(n * half, half)],
            dst_ref=kv.at[s, pl.ds(pl.multiple_of((2 + over) * blk + n * half, half), half)],
            send_sem=kv_send.at[4 + i],
            recv_sem=kv_recv.at[4 + 4 * over + i],
            device_id=(ctx_at(2 + over), h),
            device_id_type=MESH,
        )

    def relay_copy(n, s):
        i = 2 * n + s
        held = 1 + 2 * x
        return pltpu.make_async_remote_copy(
            src_ref=kv.at[s, pl.ds(pl.multiple_of(held * blk + n * half, half), half)],
            dst_ref=kv.at[s, pl.ds(2 * blk + n * half, half)],
            send_sem=kv_send.at[8 + i],
            recv_sem=kv_recv.at[4 + i],
            device_id=(ctx_at(1 - 2 * x), h),
            device_id_type=MESH,
        )

    def arrival(slot, n, s):
        here = kv.at[s, pl.ds(slot * blk + n * half, half)]
        return pltpu.make_async_copy(here, here, kv_recv.at[4 * (slot - 1) + 2 * n + s])

    pieces = [(n, s) for n in (0, 1) for s in (1, 0)]
    for n, tokens in enumerate(halves):
        total = None
        for i, part in enumerate(parts):
            if n == 0:
                w_loads[i][0].wait()
                w_loads[i][1].wait()
            h_loads[n][i].wait()
            term = jnp.dot(hbuf[tokens, part], wkvb[part, :], preferred_element_type=F32)
            total = term if total is None else total + term
        kv[1, tokens, :] = total[:, 128:].astype(BF16)
        kv[0, tokens, :] = normed(total[:, :128], gk[...], tokens).astype(BF16)
        if n == 0:
            pl.semaphore_wait(barrier, 5 + (x == 1).astype(jnp.int32) - (x == 3).astype(jnp.int32))
        for s in (1, 0):
            near_copy(n, s).start()

            @pl.when(x < 3)
            def _():
                second_copy(n, s).start()

    qsum = None
    for i, part in enumerate(parts):
        q_loads[i].wait()
        term = jnp.dot(hbuf[:, part], wqb[part, :], preferred_element_type=F32)
        qsum = term if qsum is None else qsum + term
    everyone = pl.ds(0, blk)
    for j in range(heads):
        rotated = normed(qsum[:, j * 128 : (j + 1) * 128], gq[...], everyone).astype(BF16)
        for g in range(4):
            q[g * grp + j * rows : g * grp + (j + 1) * rows, :] = rotated[g * rows : (g + 1) * rows]

    factor = np.float32(128 ** (-0.5) * np.log2(np.e))
    contract_last = (((1,), (1,)), ((), ()))

    def lane_fold(op, x):
        folded = x[:, :128]
        for i in range(1, x.shape[1] // 128):
            folded = op(folded, x[:, i * 128 : (i + 1) * 128])
        return folded

    def q_start(t):
        return jnp.where((y_hi if t >= 2 else 1 - y_hi) == 0, start[0], start[1])

    for t in range(4):
        s = lax.dot_general(
            q[t * grp : (t + 1) * grp, :], kv[0, :blk, :], contract_last,
            preferred_element_type=F32,
        )
        key = lax.broadcasted_iota(jnp.int32, (rows, blk), 1)
        k_pos = jnp.where(key < half, start[0] + key, start[1] + key - half)
        q_pos = (
            start[t // 2]
            + (t % 2) * rows
            + lax.broadcasted_iota(jnp.int32, (rows, blk), 0)
        )
        seen = k_pos <= q_pos
        for j in range(heads):
            a = pl.ds(t * grp + j * rows, rows)
            sj = jnp.where(seen, s[j * rows : (j + 1) * rows], NEG)
            m = jnp.max(lane_fold(jnp.maximum, sj), axis=-1, keepdims=True)
            p = jnp.exp2((sj - m) * factor)
            top[a, :] = jnp.broadcast_to(m, (rows, 128))
            tot[a, :] = lane_fold(jnp.add, p)
            acc[a, :] = jnp.dot(p.astype(BF16), kv[1, :blk, :], preferred_element_type=F32)

    for piece in pieces:

        @pl.when(x == 0)
        def _():
            arrival(1, *piece).wait()

        @pl.when(x == 1)
        def _():
            arrival(3, *piece).wait()

        @pl.when(x < 2)
        def _():
            relay_copy(*piece).start()

    for piece in pieces:

        @pl.when(x > 0)
        def _():
            arrival(1, *piece).wait()

        arrival(2, *piece).wait()

    mine = h * heads * 128
    results = []
    for t in range(4):
        base = pl.multiple_of(peers[t] * grp, grp)
        s = lax.dot_general(
            q[pl.ds(base, grp), :], kv[0, blk : 3 * blk, :], contract_last,
            preferred_element_type=F32,
        )
        bias = [
            jnp.where(starts[2 * ctx_at(-d) + n] <= q_start(t), np.float32(0), np.float32(NEG))
            for d in (1, 2)
            for n in (0, 1)
        ]
        for j in range(heads):
            a = pl.ds(pl.multiple_of(base + j * rows, rows), rows)
            sj = s[j * rows : (j + 1) * rows]
            quarters = [sj[:, i * half : (i + 1) * half] for i in range(4)]
            peak = functools.reduce(
                jnp.maximum, [lane_fold(jnp.maximum, x) + b for x, b in zip(quarters, bias)]
            )
            old = top[a, :]
            new = jnp.maximum(old, jnp.max(peak, axis=-1, keepdims=True))
            m = new[:, :1]
            p = jnp.concatenate(
                [jnp.exp2((x - (m - b)) * factor) for x, b in zip(quarters, bias)], axis=1
            )
            keep = jnp.exp2((old - new) * factor)
            denom = jnp.sum(tot[a, :] * keep + lane_fold(jnp.add, p), axis=-1, keepdims=True)
            value = acc[a, :] * keep + jnp.dot(
                p.astype(BF16), kv[1, blk : 3 * blk, :], preferred_element_type=F32
            )
            att[t, :, j * 128 : (j + 1) * 128] = (value * (1.0 / denom)).astype(BF16)
            target = out.at[:, pl.ds(pl.multiple_of(mine + j * 128, 128), 128)]
            if t < 3:
                copy = pltpu.make_async_remote_copy(
                    src_ref=att.at[t, :, pl.ds(j * 128, 128)],
                    dst_ref=target,
                    send_sem=out_send.at[t * heads + j],
                    recv_sem=out_recv.at[t * heads + j],
                    device_id=(c, peers[t]),
                    device_id_type=MESH,
                )
            else:
                copy = pltpu.make_async_copy(
                    att.at[t, :, pl.ds(j * 128, 128)], target, own_sem.at[j]
                )
            copy.start()
            results.append(copy)
    for piece in pieces:
        near_copy(*piece).wait_send()

        @pl.when(x < 3)
        def _():
            second_copy(*piece).wait_send()

        @pl.when(x < 2)
        def _():
            relay_copy(*piece).wait_send()

    for copy in results:
        copy.wait()


def solution(mesh):
    n_ctx = mesh.shape["ctx"]

    def shards(hidden, w_query, key_projection, value_projection, q_gain, key_norm_gain, starts):
        blk, width = hidden.shape
        cols = w_query.shape[1]
        rows = blk // 4
        freqs = (1e6 ** (-np.arange(64) * 2.0 / 128)).astype(np.float32)
        freqs = jnp.asarray(np.tile(freqs, 2).reshape(1, 128))
        any_ = pl.BlockSpec(memory_space=pl.ANY)
        vmem = pl.BlockSpec(memory_space=pltpu.VMEM)
        n_rows = rows * 4 * (cols // 128)
        return pl.pallas_call(
            functools.partial(kernel, n_ctx),
            out_shape=pltpu.VMEM((rows, cols * 4), BF16),
            in_specs=[any_] * 4 + [vmem] * 3 + [pl.BlockSpec(memory_space=pltpu.SMEM)],
            out_specs=vmem,
            scratch_shapes=[
                pltpu.VMEM((blk, width), BF16),
                pltpu.VMEM((width, cols), BF16),
                pltpu.VMEM((width, 256), BF16),
                pltpu.VMEM((blk, 128), F32),
                pltpu.VMEM((blk, 128), F32),
                pltpu.VMEM((2, 4 * blk, 128), BF16),
                pltpu.VMEM((n_rows, 128), BF16),
                pltpu.VMEM((n_rows, 128), F32),
                pltpu.VMEM((n_rows, 128), F32),
                pltpu.VMEM((n_rows, 128), F32),
                pltpu.VMEM((4, rows, cols), BF16),
                pltpu.SemaphoreType.DMA((8,)),
                pltpu.SemaphoreType.DMA((8,)),
                pltpu.SemaphoreType.DMA((4,)),
                pltpu.SemaphoreType.DMA((12,)),
                pltpu.SemaphoreType.DMA((12,)),
                pltpu.SemaphoreType.DMA((12,)),
                pltpu.SemaphoreType.DMA((12,)),
                pltpu.SemaphoreType.DMA((4,)),
            ],
            compiler_params=pltpu.CompilerParams(
                collective_id=0, has_side_effects=True, vmem_limit_bytes=60 << 20
            ),
        )(
            hidden, w_query, key_projection, value_projection,
            q_gain.reshape(1, 128), key_norm_gain.reshape(1, 128), freqs, starts,
        )

    return jax.shard_map(
        shards,
        mesh=mesh,
        in_specs=(P("ctx", None), P(None, "head"), P(None, "head"), P(None, "head"), P(), P(), P()),
        out_specs=P(("ctx", "head"), None),
        check_vma=False,
    )
```

```python
import functools

import jax
import jax.numpy as jnp
import numpy as np
from jax import lax
from jax.experimental import pallas as pl
from jax.experimental.pallas import tpu as pltpu
from jax.sharding import PartitionSpec as P

MESH = pl.DeviceIdType.MESH
NEG = -1e30
F32 = jnp.float32
BF16 = jnp.bfloat16


def half_pi_parts():
    rest, parts = np.pi / 2, []
    for _ in range(3):
        unit = 2.0 ** (np.floor(np.log2(rest)) - 7)
        parts.append(float(np.floor(rest / unit) * unit))
        rest -= parts[-1]
    return parts + [float(np.float32(rest))]


def cos_sin(angle, is_cos):
    turns = jnp.floor(angle * np.float32(2 / np.pi) + 0.5)
    r = angle
    for part in half_pi_parts():
        r = r - turns * np.float32(part)
    r2 = r * r
    s = r + r * r2 * (
        np.float32(-1.6666654611e-1)
        + r2 * (np.float32(8.3321608736e-3) + r2 * np.float32(-1.9515295891e-4))
    )
    c = 1.0 - 0.5 * r2 + r2 * r2 * (
        np.float32(4.166664568298827e-2)
        + r2 * (np.float32(-1.388731625493765e-3) + r2 * np.float32(2.443315711809948e-5))
    )
    quadrant = turns.astype(jnp.int32) + jnp.where(is_cos, 0, 3)
    value = jnp.where((quadrant & 1) == 0, c, s)
    return jnp.where(((quadrant + 1) & 2) == 0, value, -value)


def kernel(
    n_ctx, hid, wq, wk, wv, gq, gk, freq, starts, out,
    hbuf, wqb, wkvb, cosb, sinb, kt, vb, q, acc, top, tot, att,
    w_sem, h_sem, q_sem, kv_send, kv_recv, out_send, out_recv, own_sem,
):
    c = lax.axis_index("ctx")
    h = lax.axis_index("head")
    blk, width = hid.shape
    half = blk // 2
    heads = wq.shape[1] // 128
    rows = blk // 4
    grp = heads * rows
    chunks = 4
    step = width // chunks

    def ctx_at(d):
        return lax.rem(c + (d + n_ctx), n_ctx)

    x = lax.rem(c, 4)
    y_hi, core = h // 2, lax.rem(h, 2)
    peers = (
        (1 - y_hi) * 2 + core,
        (1 - y_hi) * 2 + 1 - core,
        y_hi * 2 + 1 - core,
        h,
    )

    barrier = pltpu.get_barrier_semaphore()
    for d in (-1, jnp.where(x == 0, 1, jnp.where(x == 1, -3, -2))):
        pl.semaphore_signal(barrier, inc=1, device_id=(ctx_at(d), h), device_id_type=MESH)
    for peer in peers[:3]:
        pl.semaphore_signal(barrier, inc=1, device_id=(c, peer), device_id_type=MESH)

    parts = [pl.ds(i * step, step) for i in range(chunks)]
    halves = [pl.ds(0, half), pl.ds(half, half)]
    w_loads = [
        (
            pltpu.make_async_copy(wk.at[part], wkvb.at[part, pl.ds(0, 128)], w_sem.at[2 * i]),
            pltpu.make_async_copy(wv.at[part], wkvb.at[part, pl.ds(128, 128)], w_sem.at[2 * i + 1]),
        )
        for i, part in enumerate(parts)
    ]
    h_loads = [
        [
            pltpu.make_async_copy(
                hid.at[tokens, part], hbuf.at[tokens, part], h_sem.at[n * chunks + i]
            )
            for i, part in enumerate(parts)
        ]
        for n, tokens in enumerate(halves)
    ]
    q_loads = [
        pltpu.make_async_copy(wq.at[part], wqb.at[part], q_sem.at[i])
        for i, part in enumerate(parts)
    ]
    for i in range(chunks):
        w_loads[i][0].start()
        w_loads[i][1].start()
        h_loads[0][i].start()
    for load in h_loads[1] + q_loads:
        load.start()

    lane = lax.broadcasted_iota(jnp.int32, (blk, 128), 1)
    token = lax.broadcasted_iota(jnp.int32, (blk, 128), 0)
    start = [starts[2 * c], starts[2 * c + 1]]
    pos = jnp.where(token < half, start[0] + token, start[1] + token - half)
    first = lane < 64
    table = cos_sin(pos.astype(F32) * freq[...], first)
    turned = pltpu.roll(table, 64, 1)
    cosb[...] = jnp.where(first, table, turned)
    sinb[...] = jnp.where(first, -turned, table)

    def normed(x, gain, tokens):
        x = x * lax.rsqrt(jnp.mean(x * x, axis=-1, keepdims=True) + 1e-6) * gain
        return x * cosb[tokens, :] + pltpu.roll(x, 64, 1) * sinb[tokens, :]

    def held(s, at, size):
        span = pl.ds(at if isinstance(at, int) else pl.multiple_of(at, size), size)
        return vb.at[span] if s else kt.at[:, span]

    def near_copy(n, s):
        i = 2 * n + s
        return pltpu.make_async_remote_copy(
            src_ref=held(s, n * rows, rows),
            dst_ref=held(s, blk + n * rows, rows),
            send_sem=kv_send.at[i],
            recv_sem=kv_recv.at[i],
            device_id=(ctx_at(1), h),
            device_id_type=MESH,
        )

    def second_copy(n, s):
        i = 2 * n + s
        over = (x == 2).astype(jnp.int32)
        return pltpu.make_async_remote_copy(
            src_ref=held(s, n * rows, rows),
            dst_ref=held(s, (2 + over) * blk + n * rows, rows),
            send_sem=kv_send.at[8 + i],
            recv_sem=kv_recv.at[8 + 8 * over + i],
            device_id=(ctx_at(2 + over), h),
            device_id_type=MESH,
        )

    def relay_copy(n, s):
        i = 2 * n + s
        return pltpu.make_async_remote_copy(
            src_ref=held(s, (1 + 2 * x) * blk + n * rows, rows),
            dst_ref=held(s, 2 * blk + n * rows, rows),
            send_sem=kv_send.at[16 + i],
            recv_sem=kv_recv.at[8 + i],
            device_id=(ctx_at(1 - 2 * x), h),
            device_id_type=MESH,
        )

    def arrival(slot, n, s):
        here = held(s, slot * blk + n * rows, rows)
        return pltpu.make_async_copy(here, here, kv_recv.at[8 * (slot - 1) + 2 * n + s])

    pieces = [(n, s) for n in range(4) for s in (1, 0)]
    for n, tokens in enumerate(halves):
        total = None
        for i, part in enumerate(parts):
            if n == 0:
                w_loads[i][0].wait()
                w_loads[i][1].wait()
            h_loads[n][i].wait()
            term = jnp.dot(hbuf[tokens, part], wkvb[part, :], preferred_element_type=F32)
            total = term if total is None else total + term
        vb[tokens, :] = total[:, 128:].astype(BF16)
        kt[:, tokens] = normed(total[:, :128], gk[...], tokens).T.astype(BF16)
        if n == 0:
            pl.semaphore_wait(barrier, 5 + (x == 1).astype(jnp.int32) - (x == 3).astype(jnp.int32))
        for piece in pieces[4 * n : 4 * n + 4]:
            near_copy(*piece).start()

            @pl.when(x < 3)
            def _():
                second_copy(*piece).start()

    qsum = None
    for i, part in enumerate(parts):
        q_loads[i].wait()
        term = jnp.dot(hbuf[:, part], wqb[part, :], preferred_element_type=F32)
        qsum = term if qsum is None else qsum + term
    everyone = pl.ds(0, blk)
    for j in range(heads):
        rotated = normed(qsum[:, j * 128 : (j + 1) * 128], gq[...], everyone).astype(BF16)
        for g in range(4):
            q[g * grp + j * rows : g * grp + (j + 1) * rows, :] = rotated[g * rows : (g + 1) * rows]

    factor = np.float32(128 ** (-0.5) * np.log2(np.e))

    def lane_fold(op, x):
        folded = x[:, :128]
        for i in range(1, x.shape[1] // 128):
            folded = op(folded, x[:, i * 128 : (i + 1) * 128])
        return folded

    def weights(x, tops):
        return jnp.concatenate(
            [
                jnp.exp2((x[:, i * 128 : (i + 1) * 128] - top_i) * factor)
                for i, top_i in enumerate(tops)
            ],
            axis=1,
        )

    def q_start(t):
        return jnp.where((y_hi if t >= 2 else 1 - y_hi) == 0, start[0], start[1])

    triangle = lax.broadcasted_iota(jnp.int32, (rows, 128), 1) <= lax.broadcasted_iota(
        jnp.int32, (rows, 128), 0
    )
    for t in range(4):
        mine, other = t // 2, 1 - t // 2
        tiles = t % 2 + 1
        bias = jnp.where(start[other] <= start[mine], np.float32(0), np.float32(NEG))
        k_mine = slice(mine * half, mine * half + tiles * rows)
        k_other = slice(other * half, (other + 1) * half)
        s_mine = jnp.dot(q[t * grp : (t + 1) * grp, :], kt[:, k_mine], preferred_element_type=F32)
        s_other = jnp.dot(q[t * grp : (t + 1) * grp, :], kt[:, k_other], preferred_element_type=F32)
        for j in range(heads):
            a = pl.ds(t * grp + j * rows, rows)
            sm = s_mine[j * rows : (j + 1) * rows]
            so = s_other[j * rows : (j + 1) * rows]
            edge = jnp.where(triangle, sm[:, -128:], NEG)
            sm = edge if tiles == 1 else jnp.concatenate([sm[:, :128], edge], axis=1)
            peak = jnp.maximum(lane_fold(jnp.maximum, sm), lane_fold(jnp.maximum, so) + bias)
            m = jnp.broadcast_to(jnp.max(peak, axis=-1, keepdims=True), (rows, 128))
            p_mine = weights(sm, [m] * tiles)
            p_other = weights(so, [m - bias] * (half // 128))
            top[a, :] = m
            tot[a, :] = lane_fold(jnp.add, p_mine) + lane_fold(jnp.add, p_other)
            acc[a, :] = jnp.dot(
                p_mine.astype(BF16), vb[k_mine, :], preferred_element_type=F32
            ) + jnp.dot(p_other.astype(BF16), vb[k_other, :], preferred_element_type=F32)

    for piece in pieces:

        @pl.when(x == 0)
        def _():
            arrival(1, *piece).wait()

        @pl.when(x == 1)
        def _():
            arrival(3, *piece).wait()

        @pl.when(x < 2)
        def _():
            relay_copy(*piece).start()

    for piece in pieces:

        @pl.when(x > 0)
        def _():
            arrival(1, *piece).wait()

        arrival(2, *piece).wait()

    mine = h * heads * 128
    results = []
    for t in range(4):
        base = pl.multiple_of(peers[t] * grp, grp)
        s = jnp.dot(q[pl.ds(base, grp), :], kt[:, blk : 3 * blk], preferred_element_type=F32)
        bias = [
            jnp.where(starts[2 * ctx_at(-d) + n] <= q_start(t), np.float32(0), np.float32(NEG))
            for d in (1, 2)
            for n in (0, 1)
        ]
        for j in range(heads):
            a = pl.ds(pl.multiple_of(base + j * rows, rows), rows)
            sj = s[j * rows : (j + 1) * rows]
            quarters = [sj[:, i * half : (i + 1) * half] for i in range(4)]
            peak = functools.reduce(
                jnp.maximum, [lane_fold(jnp.maximum, x) + b for x, b in zip(quarters, bias)]
            )
            old = top[a, :]
            new = jnp.maximum(old, jnp.max(peak, axis=-1, keepdims=True))
            p = weights(sj, [new - b for b in bias for _ in range(half // 128)])
            keep = jnp.exp2((old - new) * factor)
            denom = jnp.sum(tot[a, :] * keep + lane_fold(jnp.add, p), axis=-1, keepdims=True)
            value = acc[a, :] * keep + jnp.dot(
                p.astype(BF16), vb[blk : 3 * blk, :], preferred_element_type=F32
            )
            att[t, :, j * 128 : (j + 1) * 128] = (value * (1.0 / denom)).astype(BF16)
            target = out.at[:, pl.ds(pl.multiple_of(mine + j * 128, 128), 128)]
            if t < 3:
                copy = pltpu.make_async_remote_copy(
                    src_ref=att.at[t, :, pl.ds(j * 128, 128)],
                    dst_ref=target,
                    send_sem=out_send.at[t * heads + j],
                    recv_sem=out_recv.at[t * heads + j],
                    device_id=(c, peers[t]),
                    device_id_type=MESH,
                )
            else:
                copy = pltpu.make_async_copy(
                    att.at[t, :, pl.ds(j * 128, 128)], target, own_sem.at[j]
                )
            copy.start()
            results.append(copy)
    for piece in pieces:
        near_copy(*piece).wait_send()

        @pl.when(x < 3)
        def _():
            second_copy(*piece).wait_send()

        @pl.when(x < 2)
        def _():
            relay_copy(*piece).wait_send()

    for copy in results:
        copy.wait()


def solution(mesh):
    n_ctx = mesh.shape["ctx"]

    def shards(hidden, w_query, key_projection, value_projection, q_gain, key_norm_gain, starts):
        blk, width = hidden.shape
        cols = w_query.shape[1]
        rows = blk // 4
        freqs = (1e6 ** (-np.arange(64) * 2.0 / 128)).astype(np.float32)
        freqs = jnp.asarray(np.tile(freqs, 2).reshape(1, 128))
        any_ = pl.BlockSpec(memory_space=pl.ANY)
        vmem = pl.BlockSpec(memory_space=pltpu.VMEM)
        n_rows = rows * 4 * (cols // 128)
        return pl.pallas_call(
            functools.partial(kernel, n_ctx),
            out_shape=pltpu.VMEM((rows, cols * 4), BF16),
            in_specs=[any_] * 4 + [vmem] * 3 + [pl.BlockSpec(memory_space=pltpu.SMEM)],
            out_specs=vmem,
            scratch_shapes=[
                pltpu.VMEM((blk, width), BF16),
                pltpu.VMEM((width, cols), BF16),
                pltpu.VMEM((width, 256), BF16),
                pltpu.VMEM((blk, 128), F32),
                pltpu.VMEM((blk, 128), F32),
                pltpu.VMEM((128, 4 * blk), BF16),
                pltpu.VMEM((4 * blk, 128), BF16),
                pltpu.VMEM((n_rows, 128), BF16),
                pltpu.VMEM((n_rows, 128), F32),
                pltpu.VMEM((n_rows, 128), F32),
                pltpu.VMEM((n_rows, 128), F32),
                pltpu.VMEM((4, rows, cols), BF16),
                pltpu.SemaphoreType.DMA((8,)),
                pltpu.SemaphoreType.DMA((8,)),
                pltpu.SemaphoreType.DMA((4,)),
                pltpu.SemaphoreType.DMA((24,)),
                pltpu.SemaphoreType.DMA((24,)),
                pltpu.SemaphoreType.DMA((12,)),
                pltpu.SemaphoreType.DMA((12,)),
                pltpu.SemaphoreType.DMA((4,)),
            ],
            compiler_params=pltpu.CompilerParams(
                collective_id=0, has_side_effects=True, vmem_limit_bytes=60 << 20
            ),
        )(
            hidden, w_query, key_projection, value_projection,
            q_gain.reshape(1, 128), key_norm_gain.reshape(1, 128), freqs, starts,
        )

    return jax.shard_map(
        shards,
        mesh=mesh,
        in_specs=(P("ctx", None), P(None, "head"), P(None, "head"), P(None, "head"), P(), P(), P()),
        out_specs=P(("ctx", "head"), None),
        check_vma=False,
    )
```

```python
import functools

import jax
import jax.numpy as jnp
import numpy as np
from jax import lax
from jax.experimental import pallas as pl
from jax.experimental.pallas import tpu as pltpu
from jax.sharding import PartitionSpec as P

MESH = pl.DeviceIdType.MESH
NEG = -1e30
F32 = jnp.float32
BF16 = jnp.bfloat16


def half_pi_parts():
    rest, parts = np.pi / 2, []
    for _ in range(3):
        unit = 2.0 ** (np.floor(np.log2(rest)) - 7)
        parts.append(float(np.floor(rest / unit) * unit))
        rest -= parts[-1]
    return parts + [float(np.float32(rest))]


def cos_sin(angle, is_cos):
    turns = jnp.floor(angle * np.float32(2 / np.pi) + 0.5)
    r = angle
    for part in half_pi_parts():
        r = r - turns * np.float32(part)
    r2 = r * r
    s = r + r * r2 * (
        np.float32(-1.6666654611e-1)
        + r2 * (np.float32(8.3321608736e-3) + r2 * np.float32(-1.9515295891e-4))
    )
    c = 1.0 - 0.5 * r2 + r2 * r2 * (
        np.float32(4.166664568298827e-2)
        + r2 * (np.float32(-1.388731625493765e-3) + r2 * np.float32(2.443315711809948e-5))
    )
    quadrant = turns.astype(jnp.int32) + jnp.where(is_cos, 0, 3)
    value = jnp.where((quadrant & 1) == 0, c, s)
    return jnp.where(((quadrant + 1) & 2) == 0, value, -value)


def kernel(
    n_ctx, hid, wq, wk, wv, gq, gk, freq, starts, out,
    hbuf, wqb, wkvb, cosb, sinb, kt, vb, q, acc, top, tot, att,
    w_sem, h_sem, q_sem, kv_send, kv_recv, out_send, out_recv, own_sem,
):
    c = lax.axis_index("ctx")
    h = lax.axis_index("head")
    blk, width = hid.shape
    half = blk // 2
    heads = wq.shape[1] // 128
    rows = blk // 4
    grp = heads * rows
    chunks = 4
    step = width // chunks

    def ctx_at(d):
        return lax.rem(c + (d + n_ctx), n_ctx)

    x = lax.rem(c, 4)
    y_hi, core = h // 2, lax.rem(h, 2)
    peers = (
        (1 - y_hi) * 2 + core,
        (1 - y_hi) * 2 + 1 - core,
        y_hi * 2 + 1 - core,
        h,
    )

    barrier = pltpu.get_barrier_semaphore()
    for d in (-1, jnp.where(x == 0, 1, jnp.where(x == 1, -3, -2))):
        pl.semaphore_signal(barrier, inc=1, device_id=(ctx_at(d), h), device_id_type=MESH)
    for peer in peers[:3]:
        pl.semaphore_signal(barrier, inc=1, device_id=(c, peer), device_id_type=MESH)

    parts = [pl.ds(i * step, step) for i in range(chunks)]
    halves = [pl.ds(0, half), pl.ds(half, half)]
    w_loads = [
        (
            pltpu.make_async_copy(wk.at[part], wkvb.at[part, pl.ds(0, 128)], w_sem.at[2 * i]),
            pltpu.make_async_copy(wv.at[part], wkvb.at[part, pl.ds(128, 128)], w_sem.at[2 * i + 1]),
        )
        for i, part in enumerate(parts)
    ]
    h_loads = [
        [
            pltpu.make_async_copy(
                hid.at[tokens, part], hbuf.at[tokens, part], h_sem.at[n * chunks + i]
            )
            for i, part in enumerate(parts)
        ]
        for n, tokens in enumerate(halves)
    ]
    q_loads = [
        pltpu.make_async_copy(wq.at[part], wqb.at[part], q_sem.at[i])
        for i, part in enumerate(parts)
    ]
    for i in range(chunks):
        w_loads[i][0].start()
        w_loads[i][1].start()
        h_loads[0][i].start()
    for load in h_loads[1] + q_loads:
        load.start()

    lane = lax.broadcasted_iota(jnp.int32, (blk, 128), 1)
    token = lax.broadcasted_iota(jnp.int32, (blk, 128), 0)
    start = [starts[2 * c], starts[2 * c + 1]]
    pos = jnp.where(token < half, start[0] + token, start[1] + token - half)
    first = lane < 64
    table = cos_sin(pos.astype(F32) * freq[...], first)
    turned = pltpu.roll(table, 64, 1)
    cosb[...] = jnp.where(first, table, turned)
    sinb[...] = jnp.where(first, -turned, table)

    def normed(x, gain, tokens):
        x = x * lax.rsqrt(jnp.mean(x * x, axis=-1, keepdims=True) + 1e-6) * gain
        return x * cosb[tokens, :] + pltpu.roll(x, 64, 1) * sinb[tokens, :]

    def held(s, at, size):
        span = pl.ds(at if isinstance(at, int) else pl.multiple_of(at, size), size)
        return vb.at[span] if s else kt.at[:, span]

    def near_copy(n, s):
        i = 2 * n + s
        return pltpu.make_async_remote_copy(
            src_ref=held(s, n * rows, rows),
            dst_ref=held(s, blk + n * rows, rows),
            send_sem=kv_send.at[i],
            recv_sem=kv_recv.at[i],
            device_id=(ctx_at(1), h),
            device_id_type=MESH,
        )

    def second_copy(n, s):
        i = 2 * n + s
        over = (x == 2).astype(jnp.int32)
        return pltpu.make_async_remote_copy(
            src_ref=held(s, n * rows, rows),
            dst_ref=held(s, (2 + over) * blk + n * rows, rows),
            send_sem=kv_send.at[8 + i],
            recv_sem=kv_recv.at[8 + 8 * over + i],
            device_id=(ctx_at(2 + over), h),
            device_id_type=MESH,
        )

    def relay_copy(n, s):
        i = 2 * n + s
        return pltpu.make_async_remote_copy(
            src_ref=held(s, (1 + 2 * x) * blk + n * rows, rows),
            dst_ref=held(s, 2 * blk + n * rows, rows),
            send_sem=kv_send.at[16 + i],
            recv_sem=kv_recv.at[8 + i],
            device_id=(ctx_at(1 - 2 * x), h),
            device_id_type=MESH,
        )

    def arrival(slot, n, s):
        here = held(s, slot * blk + n * rows, rows)
        return pltpu.make_async_copy(here, here, kv_recv.at[8 * (slot - 1) + 2 * n + s])

    pieces = [(n, s) for n in range(4) for s in (1, 0)]
    for n, tokens in enumerate(halves):
        total = None
        for i, part in enumerate(parts):
            if n == 0:
                w_loads[i][0].wait()
                w_loads[i][1].wait()
            h_loads[n][i].wait()
            term = jnp.dot(hbuf[tokens, part], wkvb[part, :], preferred_element_type=F32)
            total = term if total is None else total + term
        vb[tokens, :] = total[:, 128:].astype(BF16)
        kt[:, tokens] = normed(total[:, :128], gk[...], tokens).T.astype(BF16)
        if n == 0:
            pl.semaphore_wait(barrier, 5 + (x == 1).astype(jnp.int32) - (x == 3).astype(jnp.int32))
        for piece in pieces[4 * n : 4 * n + 4]:
            @pl.when(x < 3)
            def _():
                second_copy(*piece).start()

            near_copy(*piece).start()

    qsum = None
    for i, part in enumerate(parts):
        q_loads[i].wait()
        term = jnp.dot(hbuf[:, part], wqb[part, :], preferred_element_type=F32)
        qsum = term if qsum is None else qsum + term
    everyone = pl.ds(0, blk)
    for j in range(heads):
        rotated = normed(qsum[:, j * 128 : (j + 1) * 128], gq[...], everyone).astype(BF16)
        for g in range(4):
            q[g * grp + j * rows : g * grp + (j + 1) * rows, :] = rotated[g * rows : (g + 1) * rows]

    factor = np.float32(128 ** (-0.5) * np.log2(np.e))

    def lane_fold(op, x):
        folded = x[:, :128]
        for i in range(1, x.shape[1] // 128):
            folded = op(folded, x[:, i * 128 : (i + 1) * 128])
        return folded

    def weights(x, tops):
        return jnp.concatenate(
            [
                jnp.exp2((x[:, i * 128 : (i + 1) * 128] - top_i) * factor)
                for i, top_i in enumerate(tops)
            ],
            axis=1,
        )

    def q_start(t):
        return jnp.where((y_hi if t >= 2 else 1 - y_hi) == 0, start[0], start[1])

    triangle = lax.broadcasted_iota(jnp.int32, (rows, 128), 1) <= lax.broadcasted_iota(
        jnp.int32, (rows, 128), 0
    )
    for t in range(4):
        mine, other = t // 2, 1 - t // 2
        tiles = t % 2 + 1
        bias = jnp.where(start[other] <= start[mine], np.float32(0), np.float32(NEG))
        k_mine = slice(mine * half, mine * half + tiles * rows)
        k_other = slice(other * half, (other + 1) * half)
        s_mine = jnp.dot(q[t * grp : (t + 1) * grp, :], kt[:, k_mine], preferred_element_type=F32)
        s_other = jnp.dot(q[t * grp : (t + 1) * grp, :], kt[:, k_other], preferred_element_type=F32)
        for j in range(heads):
            a = pl.ds(t * grp + j * rows, rows)
            sm = s_mine[j * rows : (j + 1) * rows]
            so = s_other[j * rows : (j + 1) * rows]
            edge = jnp.where(triangle, sm[:, -128:], NEG)
            sm = edge if tiles == 1 else jnp.concatenate([sm[:, :128], edge], axis=1)
            peak = jnp.maximum(lane_fold(jnp.maximum, sm), lane_fold(jnp.maximum, so) + bias)
            m = jnp.broadcast_to(jnp.max(peak, axis=-1, keepdims=True), (rows, 128))
            p_mine = weights(sm, [m] * tiles)
            p_other = weights(so, [m - bias] * (half // 128))
            top[a, :] = m
            tot[a, :] = lane_fold(jnp.add, p_mine) + lane_fold(jnp.add, p_other)
            acc[a, :] = jnp.dot(
                p_mine.astype(BF16), vb[k_mine, :], preferred_element_type=F32
            ) + jnp.dot(p_other.astype(BF16), vb[k_other, :], preferred_element_type=F32)

    for piece in pieces:

        @pl.when(x == 0)
        def _():
            arrival(1, *piece).wait()

        @pl.when(x == 1)
        def _():
            arrival(3, *piece).wait()

        @pl.when(x < 2)
        def _():
            relay_copy(*piece).start()

    for piece in pieces:

        @pl.when(x > 0)
        def _():
            arrival(1, *piece).wait()

        arrival(2, *piece).wait()

    mine = h * heads * 128
    results = []
    for t in range(4):
        base = pl.multiple_of(peers[t] * grp, grp)
        s = jnp.dot(q[pl.ds(base, grp), :], kt[:, blk : 3 * blk], preferred_element_type=F32)
        bias = [
            jnp.where(starts[2 * ctx_at(-d) + n] <= q_start(t), np.float32(0), np.float32(NEG))
            for d in (1, 2)
            for n in (0, 1)
        ]
        for j in range(heads):
            a = pl.ds(pl.multiple_of(base + j * rows, rows), rows)
            sj = s[j * rows : (j + 1) * rows]
            quarters = [sj[:, i * half : (i + 1) * half] for i in range(4)]
            peak = functools.reduce(
                jnp.maximum, [lane_fold(jnp.maximum, x) + b for x, b in zip(quarters, bias)]
            )
            old = top[a, :]
            new = jnp.maximum(old, jnp.max(peak, axis=-1, keepdims=True))
            p = weights(sj, [new - b for b in bias for _ in range(half // 128)])
            keep = jnp.exp2((old - new) * factor)
            denom = jnp.sum(tot[a, :] * keep + lane_fold(jnp.add, p), axis=-1, keepdims=True)
            value = acc[a, :] * keep + jnp.dot(
                p.astype(BF16), vb[blk : 3 * blk, :], preferred_element_type=F32
            )
            att[t, :, j * 128 : (j + 1) * 128] = (value * (1.0 / denom)).astype(BF16)
            target = out.at[:, pl.ds(pl.multiple_of(mine + j * 128, 128), 128)]
            if t < 3:
                copy = pltpu.make_async_remote_copy(
                    src_ref=att.at[t, :, pl.ds(j * 128, 128)],
                    dst_ref=target,
                    send_sem=out_send.at[t * heads + j],
                    recv_sem=out_recv.at[t * heads + j],
                    device_id=(c, peers[t]),
                    device_id_type=MESH,
                )
            else:
                copy = pltpu.make_async_copy(
                    att.at[t, :, pl.ds(j * 128, 128)], target, own_sem.at[j]
                )
            copy.start()
            results.append(copy)
    for piece in pieces:
        near_copy(*piece).wait_send()

        @pl.when(x < 3)
        def _():
            second_copy(*piece).wait_send()

        @pl.when(x < 2)
        def _():
            relay_copy(*piece).wait_send()

    for copy in results:
        copy.wait()


def solution(mesh):
    n_ctx = mesh.shape["ctx"]

    def shards(hidden, w_query, key_projection, value_projection, q_gain, key_norm_gain, starts):
        blk, width = hidden.shape
        cols = w_query.shape[1]
        rows = blk // 4
        freqs = (1e6 ** (-np.arange(64) * 2.0 / 128)).astype(np.float32)
        freqs = jnp.asarray(np.tile(freqs, 2).reshape(1, 128))
        any_ = pl.BlockSpec(memory_space=pl.ANY)
        vmem = pl.BlockSpec(memory_space=pltpu.VMEM)
        n_rows = rows * 4 * (cols // 128)
        return pl.pallas_call(
            functools.partial(kernel, n_ctx),
            out_shape=pltpu.VMEM((rows, cols * 4), BF16),
            in_specs=[any_] * 4 + [vmem] * 3 + [pl.BlockSpec(memory_space=pltpu.SMEM)],
            out_specs=vmem,
            scratch_shapes=[
                pltpu.VMEM((blk, width), BF16),
                pltpu.VMEM((width, cols), BF16),
                pltpu.VMEM((width, 256), BF16),
                pltpu.VMEM((blk, 128), F32),
                pltpu.VMEM((blk, 128), F32),
                pltpu.VMEM((128, 4 * blk), BF16),
                pltpu.VMEM((4 * blk, 128), BF16),
                pltpu.VMEM((n_rows, 128), BF16),
                pltpu.VMEM((n_rows, 128), F32),
                pltpu.VMEM((n_rows, 128), F32),
                pltpu.VMEM((n_rows, 128), F32),
                pltpu.VMEM((4, rows, cols), BF16),
                pltpu.SemaphoreType.DMA((8,)),
                pltpu.SemaphoreType.DMA((8,)),
                pltpu.SemaphoreType.DMA((4,)),
                pltpu.SemaphoreType.DMA((24,)),
                pltpu.SemaphoreType.DMA((24,)),
                pltpu.SemaphoreType.DMA((12,)),
                pltpu.SemaphoreType.DMA((12,)),
                pltpu.SemaphoreType.DMA((4,)),
            ],
            compiler_params=pltpu.CompilerParams(
                collective_id=0, has_side_effects=True, vmem_limit_bytes=60 << 20
            ),
        )(
            hidden, w_query, key_projection, value_projection,
            q_gain.reshape(1, 128), key_norm_gain.reshape(1, 128), freqs, starts,
        )

    return jax.shard_map(
        shards,
        mesh=mesh,
        in_specs=(P("ctx", None), P(None, "head"), P(None, "head"), P(None, "head"), P(), P(), P()),
        out_specs=P(("ctx", "head"), None),
        check_vma=False,
    )
```
